128 devices in a mesh: dp: 16 (over y_lo, x, core), blk: 8 (over y_hi, z).
Axes of the slice: x: 4, y: 4 (y_hi: 2, y_lo: 2; y = y_hi * 2 + y_lo), z: 4, core: 2. Of those that a mesh axis runs over, the one named last changes fastest.
Arguments:
- tokens: bfloat16 [1024, 3072], P('blk'), may hold values from -6 to 6
- expert_ids: int32 [1024, 2], P('blk'), may hold values from 0 to 7, all different within a row; in each aligned block of 128 rows (0 to 127, 128 to 255, ...) at most 64 rows name the same one
- gate_levels: int32 [1024, 2], P('blk'), may hold values from 1 to 255
- out_grad: bfloat16 [1024, 3072], P('blk'), may hold values from -6 to 6
- panels: bfloat16 [8, 2, 3072, 8192], P('blk', None, None, 'dp'), may hold values from -0.109375 to 0.109375
Outputs:
- token_grad: bfloat16 [1024, 3072], P('blk', 'dp')
- panel_grads: float32 [8, 2, 3072, 8192], P('blk', None, None, 'dp')
The draws below stay inside these ranges and needn't reach their ends.
Inputs may be any that keep to these rules, and one draw needn't show every extreme that they name: `expert_ids`: the 2 experts of a token differ; among the 128 tokens of one index of blk no expert is chosen more than 64 times, and some expert is chosen exactly 64 times on some indices.
All inputs are finite; a program needn't handle non-finite values.
Results may differ from the reference program's by a relative error of at most 0.0058.
Values may be sent and summed in bfloat16 or wider, within the bound.
No kernel may reach another device: no remote copies, remote signals or barrier semaphores. Data moves between devices by JAX's collectives and lax.ppermute only.
A program may use at most 128 MiB of HBM per device.

```python
import math
import jax
import jax.numpy as jnp
import numpy as np
from jax import lax

D = 3072
HID = 8192
TOP = 2
TOK_DEV = 128
EXPERTS = 8
CAP = 64
TOKENS = 1024
N_BLK = 8


def plant(result, stream_key, smallest, top_value):
    place = [jax.random.randint(jax.random.fold_in(stream_key, axis), (), 0, length) for axis, length in enumerate(result.shape)]
    main_axis = result.shape.index(max(result.shape))
    next_to = place[:main_axis] + [(place[main_axis] + 1) % result.shape[main_axis]] + place[main_axis + 1:]
    return result.at[tuple(place)].set(smallest).at[tuple(next_to)].set(top_value)


def levels(rng, shape, cuts, smallest, top_value):
    def one(position, parts):
        heights = jax.random.uniform(jax.random.fold_in(jax.random.fold_in(rng, 6), position), (parts,), jnp.float32, smallest / len(cuts), top_value / len(cuts))
        return jnp.repeat(jnp.exp(heights), shape[position] // parts).reshape((-1,) + (1,) * (len(shape) - position - 1))

    level = one(*cuts[0])
    for cut in cuts[1:]:
        level = level * one(*cut)
    return level


def routed_block(stream_key, own, number, rows, number_of, top, limit, skew):
    sequence = jax.random.permutation(stream_key, number_of)
    packed, usual = load_shares(number_of, rows * top, limit, skew, True), load_shares(number_of, rows * top, limit, skew, False)
    places = jnp.arange(number_of)

    def named(lengths, turn):
        used = int((lengths > 0).sum())
        fixed = max(1, used // 4)
        moved = fixed + (places - fixed + turn * (used - fixed)) % max(1, number_of - fixed)
        return jnp.zeros((number_of,), jnp.int32).at[sequence[jnp.where(places < fixed, places, moved)]].set(jnp.asarray(lengths, jnp.int32))

    lengths = jnp.where(number % 4 == 0, named(packed, number // 4), named(usual, number - number // 4 - 1))
    mixed = jax.random.permutation(jax.random.fold_in(own, 3), number_of)
    donor, receiver = mixed[0:number_of // 2 * 2:2], mixed[1:number_of // 2 * 2:2]
    margin = jnp.minimum(lengths[donor] - 1, limit - lengths[receiver]) // 2
    margin = jnp.where((donor == sequence[0]) | (receiver == sequence[0]) | (lengths[receiver] == 0), 0, jnp.maximum(margin, 0))
    moved = jax.random.randint(jax.random.fold_in(own, 4), (number_of // 2,), 0, 1 << 20) % (margin + 1)
    lengths = lengths.at[donor].add(-moved).at[receiver].add(moved)
    members = jnp.searchsorted(jnp.cumsum(lengths), jnp.arange(rows * top), side="right").astype(jnp.int32)
    listing = members.reshape(top, rows).T
    listing = listing[jax.random.permutation(jax.random.fold_in(own, 1), rows)]
    turn = jax.random.randint(jax.random.fold_in(own, 2), (rows, 1), 0, top)
    return jnp.take_along_axis(listing, (jnp.arange(top)[None, :] + turn) % top, axis=1)


def load_shares(number_of, total, limit, lean, full):
    portions = [(1 << 20) // math.isqrt(standing ** lean) + 1 for standing in range(1, number_of + 1)]
    largest = limit if full else min(limit, max(-(-total // number_of), total * portions[0] // sum(portions)))
    least = 1 if total - largest >= number_of - 1 else 0
    holding, spare = [largest] + [least] * (number_of - 1), total - largest - least * (number_of - 1)
    while spare > 0:
        candidates = [i for i in range(1, number_of) if holding[i] < largest] or [i for i in range(1, number_of) if holding[i] < limit]
        mass, budget = sum([portions[i] for i in candidates]), spare
        for i in candidates:
            addition = min(limit - holding[i], max(1, budget * portions[i] // mass), spare)
            holding[i] = holding[i] + addition
            spare = spare - addition
    return np.array(holding)


def noise(rng, extent, spread, reach, shards=(), held_as=jnp.bfloat16):
    array = jax.random.normal(rng, extent, jnp.float32) * spread
    if len(shards) > 0:
        array = levels(rng, extent, shards, -0.22, 0.18) * array
    return jnp.clip(array, min=-reach, max=reach).astype(held_as)


def setup_inputs(seed: int = 0) -> dict:
    splits = jax.random.split(jax.random.key(seed), 6)
    tokens = noise(splits[0], (TOKENS, D), 1.0, 6.0, ((0, 8),))
    expert_ids_keys = jax.random.split(jax.random.fold_in(splits[1], 1), TOKENS // TOK_DEV)
    expert_ids_turns = jax.random.permutation(jax.random.fold_in(splits[1], 3), TOKENS // TOK_DEV)
    expert_ids = jax.vmap(lambda own, number: routed_block(jax.random.fold_in(splits[1], 2), own, number, TOK_DEV, EXPERTS, TOP, CAP, 2))(expert_ids_keys, expert_ids_turns).reshape((TOKENS, TOP))
    gate_levels = plant(jax.random.randint(splits[2], (TOKENS, TOP), 1, 256), jax.random.fold_in(splits[2], 1), 1, 255).astype(jnp.int32)
    out_grad = noise(splits[3], (TOKENS, D), 1.0, 6.0, ((0, 8),))
    panels = noise(splits[4], (EXPERTS, 2, D, HID), D ** -0.5, 0.109375, ((0, 8), (3, 16)))
    return {"tokens": tokens, "expert_ids": expert_ids, "gate_levels": gate_levels, "out_grad": out_grad, "panels": panels}


def slot_tables(expert_ids, gate_levels, tok_count, num_experts, capacity):
    gate_frac = gate_levels.astype(jnp.float32)
    gate_frac = gate_frac / jnp.sum(gate_frac, axis=1, keepdims=True)
    flat_ids = expert_ids.reshape(-1).astype(jnp.int32)
    one_hot = (flat_ids[:, None] == jnp.arange(num_experts, dtype=jnp.int32)[None, :]).astype(jnp.int32)
    earlier = jnp.cumsum(one_hot, axis=0) - one_hot
    slot_pos = jnp.sum(earlier * one_hot, axis=1).astype(jnp.int32)
    top_count = expert_ids.shape[1]
    owner_tok = (jnp.arange(flat_ids.shape[0], dtype=jnp.int32) // top_count).astype(jnp.int32)
    slot_table = jnp.full((num_experts, capacity), tok_count, jnp.int32).at[flat_ids, slot_pos].set(owner_tok)
    slot_gate = jnp.zeros((num_experts, capacity), jnp.float32).at[flat_ids, slot_pos].set(gate_frac.reshape(-1))
    return slot_table, slot_gate


def dispatch(tokens, out_grad, slot_table, slot_gate):
    model_dim = tokens.shape[1]
    pad_row = jnp.zeros((1, model_dim), tokens.dtype)
    x_rows = jnp.concatenate([tokens, pad_row], axis=0)[slot_table]
    d_full = jnp.concatenate([out_grad, pad_row], axis=0)[slot_table]
    d_rows = (slot_gate[:, :, None] * d_full.astype(jnp.float32)).astype(jnp.bfloat16)
    return x_rows, d_rows


def per_expert(pieces):
    x_e, d_e, panel = pieces
    w_up = panel[0]
    w_down = panel[1]
    pre_act = jnp.dot(x_e, w_up, preferred_element_type=jnp.float32)
    sigma_act = jax.nn.sigmoid(pre_act)
    hidden = (pre_act * sigma_act).astype(jnp.bfloat16)
    back_h = jnp.dot(d_e, w_down, preferred_element_type=jnp.float32)
    d_pre = (back_h * sigma_act * (1.0 + pre_act * (1.0 - sigma_act))).astype(jnp.bfloat16)
    dx_rows = jnp.dot(d_pre, w_up.T, preferred_element_type=jnp.float32)
    grad_up = jnp.dot(x_e.T, d_pre, preferred_element_type=jnp.float32)
    grad_down = jnp.dot(d_e.T, hidden, preferred_element_type=jnp.float32)
    return dx_rows, jnp.stack([grad_up, grad_down], axis=0)


def reference(tokens, expert_ids, gate_levels, out_grad, panels):
    tok_blocks = tokens.reshape(N_BLK, TOK_DEV, D)
    grad_blocks = out_grad.reshape(N_BLK, TOK_DEV, D)
    ids_blocks = expert_ids.reshape(N_BLK, TOK_DEV, TOP)
    level_blocks = gate_levels.reshape(N_BLK, TOK_DEV, TOP)
    slot_table, slot_gate = jax.vmap(lambda ids, lev: slot_tables(ids, lev, TOK_DEV, EXPERTS, CAP))(ids_blocks, level_blocks)
    x_rows, d_rows = jax.vmap(dispatch)(tok_blocks, grad_blocks, slot_table, slot_gate)
    x_by = jnp.transpose(x_rows, (1, 0, 2, 3)).reshape(EXPERTS, N_BLK * CAP, D)
    d_by = jnp.transpose(d_rows, (1, 0, 2, 3)).reshape(EXPERTS, N_BLK * CAP, D)
    dx_all, grads = lax.map(per_expert, (x_by, d_by, panels))
    dx_blocks = jnp.transpose(dx_all.reshape(EXPERTS, N_BLK, CAP, D), (1, 0, 2, 3))

    def gather_back(table, rows):
        summed = jnp.zeros((TOK_DEV + 1, D), jnp.float32).at[table.reshape(-1)].add(rows.reshape(-1, D))
        return summed[:TOK_DEV]

    token_grad = jax.vmap(gather_back)(slot_table, dx_blocks).reshape(TOKENS, D).astype(jnp.bfloat16)
    return token_grad, grads / jnp.float32(N_BLK)
```

```python
import jax
import jax.numpy as jnp
from jax import lax
from jax.experimental import pallas as pl
from jax.experimental.pallas import tpu as pltpu
from jax.sharding import Mesh, PartitionSpec as P

EXPERTS, CAP, TOK, D, HID = 8, 64, 128, 3072, 512
ROWS = EXPERTS * CAP
HALF = D // 2
STEP = 512
HALF_STEPS = HALF // STEP
CHIPS = 8
SLICE = D // (2 * CHIPS)
BF, F32 = jnp.bfloat16, jnp.float32
BLK = ("yhi", "z")
LIMIT = 48 * 1024 * 1024


def matmul(a, b, ca, cb):
    return lax.dot_general(a, b, (((ca,), (cb,)), ((), ())), preferred_element_type=F32)


def one_hot_rows(ids_ref, lev_ref, with_gate):
    id0, id1 = ids_ref[0:1, :], ids_ref[1:2, :]
    expert = lax.broadcasted_iota(jnp.int32, (EXPERTS, TOK), 0)
    chosen = (expert == id0) | (expert == id1)
    before = lax.broadcasted_iota(jnp.int32, (TOK, TOK), 0) < lax.broadcasted_iota(
        jnp.int32, (TOK, TOK), 1
    )
    chosen_f = jnp.where(chosen, 1.0, 0.0).astype(F32)
    before_f = jnp.where(before, 1.0, 0.0).astype(F32)
    earlier = matmul(chosen_f.astype(BF), before_f.astype(BF), 1, 0)
    slot = jnp.where(chosen, earlier, -1.0)
    place = lax.broadcasted_iota(jnp.int32, (CAP, TOK), 0).astype(F32)
    hot = jnp.concatenate(
        [jnp.where(place == slot[e : e + 1, :], 1.0, 0.0).astype(F32) for e in range(EXPERTS)],
        axis=0,
    )
    if not with_gate:
        return hot.astype(BF), None
    lev0, lev1 = lev_ref[0:1, :].astype(F32), lev_ref[1:2, :].astype(F32)
    total = lev0 + lev1
    frac = jnp.where(expert == id0, lev0 / total, jnp.where(expert == id1, lev1 / total, 0.0))
    gate = jnp.concatenate(
        [
            jnp.sum(hot[e * CAP : (e + 1) * CAP, :] * frac[e : e + 1, :], axis=1, keepdims=True)
            for e in range(EXPERTS)
        ],
        axis=0,
    )
    return hot.astype(BF), gate


def dispatch_x(core, ids, tokens):
    def body(core_ref, ids_ref, tok_ref, out_ref, hot_ref):
        @pl.when(pl.program_id(0) == 0)
        def _():
            hot_ref[...] = one_hot_rows(ids_ref, None, False)[0]

        out_ref[...] = matmul(hot_ref[...], tok_ref[...], 1, 0).astype(BF)

    return pl.pallas_call(
        body,
        grid_spec=pltpu.PrefetchScalarGridSpec(
            num_scalar_prefetch=1,
            grid=(HALF_STEPS,),
            in_specs=[
                pl.BlockSpec((2, TOK), lambda i, c: (0, 0)),
                pl.BlockSpec((TOK, STEP), lambda i, c: (0, c[0] * HALF_STEPS + i)),
            ],
            out_specs=[
                pl.BlockSpec((ROWS, STEP), lambda i, c: (0, i)),
                pl.BlockSpec((ROWS, TOK), lambda i, c: (0, 0)),
            ],
        ),
        out_shape=[
            jax.ShapeDtypeStruct((ROWS, HALF), BF),
            jax.ShapeDtypeStruct((ROWS, TOK), BF),
        ],
        compiler_params=pltpu.CompilerParams(vmem_limit_bytes=LIMIT),
    )(core, ids, tokens)


def dispatch_d(core, ids, lev, out_grad):
    def body(core_ref, ids_ref, lev_ref, grad_ref, out_ref, hot_ref, gate_ref):
        @pl.when(pl.program_id(0) == 0)
        def _():
            hot, gate = one_hot_rows(ids_ref, lev_ref, True)
            hot_ref[...] = hot
            gate_ref[...] = jnp.broadcast_to(gate, (ROWS, TOK))

        rows = matmul(hot_ref[...], grad_ref[...], 1, 0)
        out_ref[...] = (rows * gate_ref[:, 0:1]).astype(BF)

    return pl.pallas_call(
        body,
        grid_spec=pltpu.PrefetchScalarGridSpec(
            num_scalar_prefetch=1,
            grid=(HALF_STEPS,),
            in_specs=[
                pl.BlockSpec((2, TOK), lambda i, c: (0, 0)),
                pl.BlockSpec((2, TOK), lambda i, c: (0, 0)),
                pl.BlockSpec((TOK, STEP), lambda i, c: (0, c[0] * HALF_STEPS + i)),
            ],
            out_specs=pl.BlockSpec((ROWS, STEP), lambda i, c: (0, i)),
            scratch_shapes=[pltpu.VMEM((ROWS, TOK), BF), pltpu.VMEM((ROWS, TOK), F32)],
        ),
        out_shape=jax.ShapeDtypeStruct((ROWS, HALF), BF),
        compiler_params=pltpu.CompilerParams(vmem_limit_bytes=LIMIT),
    )(core, ids, lev, out_grad)


def natural(k, c):
    return jnp.where(
        k < HALF_STEPS, c * HALF_STEPS + k, (1 - c) * HALF_STEPS + k - HALF_STEPS
    )


def own_block(k):
    return jnp.minimum(k, HALF_STEPS - 1)


def oth_block(k):
    return jnp.clip(k - HALF_STEPS, 0, HALF_STEPS - 1)


def forward_up(core, x_own, x_oth, panels):
    def body(core_ref, own_ref, oth_ref, w_ref, hid_ref, slope_ref, acc_ref):
        k = pl.program_id(0)

        @pl.when(k == 0)
        def _():
            acc_ref[...] = matmul(own_ref[...], w_ref[0, 0], 1, 0)

        @pl.when((k > 0) & (k < HALF_STEPS))
        def _():
            acc_ref[...] += matmul(own_ref[...], w_ref[0, 0], 1, 0)

        @pl.when(k >= HALF_STEPS)
        def _():
            acc_ref[...] += matmul(oth_ref[...], w_ref[0, 0], 1, 0)

        @pl.when(k == 2 * HALF_STEPS - 1)
        def _():
            pre = acc_ref[...]
            sig = jax.nn.sigmoid(pre)
            hid_ref[...] = (pre * sig).astype(BF)
            slope_ref[...] = sig * (1.0 + pre * (1.0 - sig))

    return pl.pallas_call(
        body,
        grid_spec=pltpu.PrefetchScalarGridSpec(
            num_scalar_prefetch=1,
            grid=(2 * HALF_STEPS,),
            in_specs=[
                pl.BlockSpec((ROWS, STEP), lambda k, c: (0, own_block(k))),
                pl.BlockSpec((ROWS, STEP), lambda k, c: (0, oth_block(k))),
                pl.BlockSpec((1, 1, STEP, HID), lambda k, c: (0, 0, natural(k, c[0]), 0)),
            ],
            out_specs=[
                pl.BlockSpec((ROWS, HID), lambda k, c: (0, 0)),
                pl.BlockSpec((ROWS, HID), lambda k, c: (0, 0)),
            ],
            scratch_shapes=[pltpu.VMEM((ROWS, HID), F32)],
        ),
        out_shape=[
            jax.ShapeDtypeStruct((ROWS, HID), BF),
            jax.ShapeDtypeStruct((ROWS, HID), F32),
        ],
        compiler_params=pltpu.CompilerParams(vmem_limit_bytes=LIMIT),
    )(core, x_own, x_oth, panels)


DX_PARTS = 4
DX_STEPS = CHIPS // DX_PARTS


def back_down(core, d_own, d_oth, slope, panels):
    back_steps = 2 * HALF_STEPS

    def body(core_ref, own_ref, oth_ref, slope_ref, wd_ref, u0, u1, u2, u3, dpre_ref, dx_ref, acc_ref):
        k = pl.program_id(0)

        @pl.when(k == 0)
        def _():
            acc_ref[...] = matmul(own_ref[...], wd_ref[0, 0], 1, 0)

        @pl.when((k > 0) & (k < HALF_STEPS))
        def _():
            acc_ref[...] += matmul(own_ref[...], wd_ref[0, 0], 1, 0)

        @pl.when((k >= HALF_STEPS) & (k < back_steps))
        def _():
            acc_ref[...] += matmul(oth_ref[...], wd_ref[0, 0], 1, 0)

        @pl.when(k == back_steps - 1)
        def _():
            dpre_ref[...] = (acc_ref[...] * slope_ref[...]).astype(BF)

        @pl.when(k >= back_steps)
        def _():
            w = jnp.concatenate([u[0, 0] for u in (u0, u1, u2, u3)], axis=0)
            dx_ref[...] = matmul(dpre_ref[...], w, 1, 1).astype(BF)

    def up_map(q):
        def index(k, c):
            step = jnp.clip(k - back_steps, 0, DX_STEPS - 1)
            return (0, 0, (step * DX_PARTS + q) * 2 + 1 - c[0], 0)

        return index

    def bk(k):
        return jnp.minimum(k, back_steps - 1)

    return pl.pallas_call(
        body,
        grid_spec=pltpu.PrefetchScalarGridSpec(
            num_scalar_prefetch=1,
            grid=(back_steps + DX_STEPS,),
            in_specs=[
                pl.BlockSpec((ROWS, STEP), lambda k, c: (0, own_block(k))),
                pl.BlockSpec((ROWS, STEP), lambda k, c: (0, oth_block(k))),
                pl.BlockSpec((ROWS, HID), lambda k, c: (0, 0)),
                pl.BlockSpec((1, 1, STEP, HID), lambda k, c: (0, 1, natural(bk(k), c[0]), 0)),
            ]
            + [pl.BlockSpec((1, 1, SLICE, HID), up_map(q)) for q in range(DX_PARTS)],
            out_specs=[
                pl.BlockSpec((ROWS, HID), lambda k, c: (0, 0)),
                pl.BlockSpec(
                    (ROWS, DX_PARTS * SLICE),
                    lambda k, c: (0, jnp.clip(k - back_steps, 0, DX_STEPS - 1)),
                ),
            ],
            scratch_shapes=[pltpu.VMEM((ROWS, HID), F32)],
        ),
        out_shape=[
            jax.ShapeDtypeStruct((ROWS, HID), BF),
            jax.ShapeDtypeStruct((ROWS, HALF), BF),
        ],
        compiler_params=pltpu.CompilerParams(vmem_limit_bytes=LIMIT),
    )(core, d_own, d_oth, slope, panels, panels, panels, panels, panels)


def dx_mine(core, d_pre, panels):
    def body(core_ref, dpre_ref, u0, u1, u2, u3, dx_ref):
        w = jnp.concatenate([u[0, 0] for u in (u0, u1, u2, u3)], axis=0)
        dx_ref[...] = matmul(dpre_ref[...], w, 1, 1)

    def up_map(q):
        return lambda k, c: (0, 0, (k * DX_PARTS + q) * 2 + c[0], 0)

    return pl.pallas_call(
        body,
        grid_spec=pltpu.PrefetchScalarGridSpec(
            num_scalar_prefetch=1,
            grid=(DX_STEPS,),
            in_specs=[pl.BlockSpec((ROWS, HID), lambda k, c: (0, 0))]
            + [pl.BlockSpec((1, 1, SLICE, HID), up_map(q)) for q in range(DX_PARTS)],
            out_specs=pl.BlockSpec((ROWS, DX_PARTS * SLICE), lambda k, c: (0, k)),
        ),
        out_shape=jax.ShapeDtypeStruct((ROWS, HALF), F32),
        compiler_params=pltpu.CompilerParams(vmem_limit_bytes=LIMIT),
    )(core, d_pre, panels, panels, panels, panels)


def weight_grads(core, x_own, x_oth, d_own, d_oth, d_pre, hidden):
    def body(core_ref, xo, xt, do, dt, dpre_ref, hid_ref, out_ref):
        g, k = pl.program_id(0), pl.program_id(1)
        cases = (
            (0, True, xo, dpre_ref),
            (0, False, xt, dpre_ref),
            (1, True, do, hid_ref),
            (1, False, dt, hid_ref),
        )
        for which, own, lhs, rhs in cases:

            @pl.when((g == which) & ((k < HALF_STEPS) == own))
            def _(lhs=lhs, rhs=rhs):
                out_ref[0, 0] = matmul(lhs[...], rhs[...], 0, 0) * (1.0 / EXPERTS)

    last = HALF_STEPS - 1

    def at(own, which):
        def index(g, k, c):
            block = own_block(k) if own else oth_block(k)
            return (0, jnp.where(g == which, block, last if which == 0 else 0))

        return pl.BlockSpec((ROWS, STEP), index)

    whole = pl.BlockSpec((ROWS, HID), lambda g, k, c: (0, 0))
    return pl.pallas_call(
        body,
        grid_spec=pltpu.PrefetchScalarGridSpec(
            num_scalar_prefetch=1,
            grid=(2, 2 * HALF_STEPS),
            in_specs=[at(True, 0), at(False, 0), at(True, 1), at(False, 1), whole, whole],
            out_specs=pl.BlockSpec(
                (1, 1, STEP, HID), lambda g, k, c: (0, g, natural(k, c[0]), 0)
            ),
        ),
        out_shape=jax.ShapeDtypeStruct((1, 2, D, HID), F32),
        compiler_params=pltpu.CompilerParams(vmem_limit_bytes=LIMIT),
        cost_estimate=pl.CostEstimate(
            flops=4 * ROWS * D * HID, transcendentals=0, bytes_accessed=8 * D * HID + 4 * ROWS * D
        ),
    )(core, x_own, x_oth, d_own, d_oth, d_pre, hidden)


def shards(tokens, expert_ids, gate_levels, out_grad, panels):
    core = lax.axis_index("core").astype(jnp.int32).reshape(1)
    ids, lev = expert_ids.T, gate_levels.T
    swap = [(0, 1), (1, 0)]

    def to_experts(rows):
        rows = rows.reshape(EXPERTS, CAP, HALF)
        own = lax.all_to_all(rows, BLK, split_axis=0, concat_axis=0, tiled=True)
        own = own.reshape(ROWS, HALF)
        return own, lax.ppermute(own, "core", swap)

    x_rows, hot = dispatch_x(core, ids, tokens)
    d_rows = dispatch_d(core, ids, lev, out_grad)
    x_own, x_oth = to_experts(x_rows)
    d_own, d_oth = to_experts(d_rows)
    hidden, slope = forward_up(core, x_own, x_oth, panels)
    d_pre, dx_send = back_down(core, d_own, d_oth, slope, panels)
    dx_recv = lax.ppermute(dx_send, "core", swap)
    dx_own = dx_mine(core, d_pre, panels)
    chip_dx = (dx_own + dx_recv.astype(F32)).astype(BF).reshape(EXPERTS, CAP, HALF)
    back = lax.all_to_all(chip_dx, BLK, split_axis=0, concat_axis=0, tiled=True)
    panel_grads = weight_grads(core, x_own, x_oth, d_own, d_oth, d_pre, hidden)
    tok_t = matmul(back.reshape(ROWS, HALF), hot, 0, 0).astype(BF)
    parts = lax.all_to_all(
        tok_t.reshape(CHIPS, SLICE, TOK), ("ylo", "x"), split_axis=0, concat_axis=0, tiled=True
    )
    token_grad = jnp.sum(parts.astype(F32), axis=0).T.astype(BF)
    return token_grad, panel_grads


def solution(mesh):
    fine = Mesh(mesh.devices.reshape(2, 4, 2, 2, 4), ("ylo", "x", "core", "yhi", "z"))
    dp = ("ylo", "x", "core")
    rows = P(BLK, None)
    return jax.shard_map(
        shards,
        mesh=fine,
        in_specs=(rows, rows, rows, rows, P(BLK, None, None, dp)),
        out_specs=(P(BLK, dp), P(BLK, None, None, dp)),
        check_vma=False,
    )
```

```python
import jax
import jax.numpy as jnp
from jax import lax
from jax.experimental import pallas as pl
from jax.experimental.pallas import tpu as pltpu
from jax.sharding import Mesh, PartitionSpec as P

EXPERTS, CAP, TOK, D, HID = 8, 64, 128, 3072, 512
ROWS = EXPERTS * CAP
HALF = D // 2
XS = 4
QUART = HALF // XS
CHIPS = 8
SLICE = D // (2 * CHIPS)
LANES = 128
REST = SLICE - LANES
PACK = CAP * SLICE // LANES
DESTS = EXPERTS * CHIPS
BF, F32 = jnp.bfloat16, jnp.float32
BLK = ("yhi", "z")
AXES = ("ylo", "x", "core", "yhi", "z")
SIZES = (2, 4, 2, 2, 4)
MIB = 1024 * 1024


def matmul(a, b, ca, cb):
    return lax.dot_general(a, b, (((ca,), (cb,)), ((), ())), preferred_element_type=F32)


VM = pl.BlockSpec(memory_space=pltpu.VMEM)
SM = pl.BlockSpec(memory_space=pltpu.SMEM)
HB = pl.BlockSpec(memory_space=pltpu.HBM)
ANY = pl.BlockSpec(memory_space=pl.ANY)
DMA = pltpu.SemaphoreType.DMA


def call(body, ins, outs, scratch, limit=20, flops=0, nbytes=0, **kw):
    return pl.pallas_call(
        body,
        in_specs=ins,
        out_specs=[VM] * len(outs),
        out_shape=[jax.ShapeDtypeStruct(s, t) for s, t in outs],
        scratch_shapes=scratch,
        compiler_params=pltpu.CompilerParams(vmem_limit_bytes=limit * MIB),
        cost_estimate=pl.CostEstimate(flops=flops, transcendentals=0, bytes_accessed=nbytes),
        **kw,
    )


def slot_rows(table):
    expert = lax.broadcasted_iota(jnp.int32, (EXPERTS, TOK), 0)
    chosen = (expert == table[0:1, :]) | (expert == table[1:2, :])
    before = lax.broadcasted_iota(jnp.int32, (TOK, TOK), 0) < lax.broadcasted_iota(
        jnp.int32, (TOK, TOK), 1
    )
    earlier = matmul(
        jnp.where(chosen, 1.0, 0.0).astype(BF), jnp.where(before, 1.0, 0.0).astype(BF), 1, 0
    )
    return expert, jnp.where(chosen, earlier, -1.0)


def hot_chunk(slot, e):
    place = lax.broadcasted_iota(jnp.int32, (CAP, TOK), 0).astype(F32)
    return jnp.where(place == slot[e : e + 1, :], 1.0, 0.0).astype(F32)


def dispatch_x(table, tokens):
    def body(table_ref, tok_ref, out_ref, hot_ref):
        _, slot = slot_rows(table_ref[...])
        for e in range(EXPERTS):
            hot_ref[e * CAP : (e + 1) * CAP, :] = hot_chunk(slot, e).astype(BF)
        out_ref[...] = matmul(hot_ref[...], tok_ref[...], 1, 0).astype(BF)

    return call(body, [VM, VM], [((ROWS, HALF), BF), ((ROWS, TOK), BF)], [])(table, tokens)


def dispatch_d(table, out_grad):
    def body(table_ref, grad_ref, out_ref, hot_ref, gate_ref):
        table = table_ref[...]
        expert, slot = slot_rows(table)
        lev = table[2:4, :].astype(F32)
        frac = lev / (lev[0:1, :] + lev[1:2, :])
        frac = jnp.where(
            expert == table[0:1, :],
            frac[0:1, :],
            jnp.where(expert == table[1:2, :], frac[1:2, :], 0.0),
        )
        for e in range(EXPERTS):
            rows = slice(e * CAP, (e + 1) * CAP)
            hot = hot_chunk(slot, e)
            hot_ref[rows, :] = hot.astype(BF)
            gate = jnp.sum(hot * frac[e : e + 1, :], axis=1, keepdims=True)
            gate_ref[rows, :] = jnp.broadcast_to(gate, (CAP, LANES))
        rows = matmul(hot_ref[...], grad_ref[...], 1, 0)
        out_ref[...] = (rows * gate_ref[:, 0:1]).astype(BF)

    return call(
        body,
        [VM, VM],
        [((ROWS, QUART), BF)],
        [pltpu.VMEM((ROWS, TOK), BF), pltpu.VMEM((ROWS, LANES), F32)],
    )(table, out_grad)[0]


def assemble(pieces):
    def body(*refs):
        for r in range(XS):
            refs[XS][:, r * QUART : (r + 1) * QUART] = refs[r][...]

    return call(body, [VM] * XS, [((ROWS, HALF), BF)], [])(*pieces)[0]


TIGHT = 59


def panel_rows(panel_ref, which, start, unit, count, buf, into, sem):
    rows = pl.ds(pl.multiple_of(start, unit), count)
    copy = pltpu.make_async_copy(panel_ref.at[0, which, rows, :], buf.at[pl.ds(into, count), :], sem)
    copy.start()
    return copy


def owned_rows(panel_ref, o, buf, sems):
    copies = []
    for j in range(CHIPS):
        first = (2 * j + o) * SLICE
        copies.append(panel_rows(panel_ref, 0, first, 64, LANES, buf, j * LANES, sems.at[2 * j]))
        copies.append(
            panel_rows(
                panel_ref, 0, first + LANES, 64, REST, buf, CHIPS * LANES + j * REST, sems.at[2 * j + 1]
            )
        )
    return copies


PARTS = 3
PART = HALF // PARTS


def half_rows(panel_ref, o, buf, sems):
    return [
        panel_rows(panel_ref, 0, o * HALF + i * PART, PART, PART, buf, i * PART, sems.at[i])
        for i in range(PARTS)
    ]


def back_full(place, d_own, d_oth, panels):
    def body(place_ref, own_ref, oth_ref, panel_ref, out_ref, buf, sems):
        copies = []
        for side in range(2):
            o = (place_ref[0] + side) % 2
            for r in range(XS):
                start = (o * XS + (place_ref[1] + XS - r) % XS) * QUART
                i = side * XS + r
                copies.append(
                    panel_rows(panel_ref, 1, start, QUART, QUART, buf, i * QUART, sems.at[i])
                )
        for c in copies[:XS]:
            c.wait()
        own = matmul(own_ref[...], buf[:HALF, :], 1, 0)
        for c in copies[XS:]:
            c.wait()
        out_ref[...] = own + matmul(oth_ref[...], buf[HALF:, :], 1, 0)

    return call(
        body,
        [SM, VM, VM, HB],
        [((ROWS, HID), F32)],
        [pltpu.VMEM((D, HID), BF), DMA((2 * XS,))],
        limit=TIGHT,
        flops=2 * ROWS * D * HID,
        nbytes=2 * D * HID,
    )(place, d_own, d_oth, panels)[0]


def up_own(place, x_own, panels):
    def body(place_ref, own_ref, panel_ref, out_ref, buf, sems):
        for c in half_rows(panel_ref, place_ref[0], buf, sems):
            c.wait()
        out_ref[...] = matmul(own_ref[...], buf[...], 1, 0)

    return call(
        body,
        [SM, VM, HB],
        [((ROWS, HID), F32)],
        [pltpu.VMEM((HALF, HID), BF), DMA((PARTS,))],
        limit=TIGHT,
        flops=ROWS * D * HID,
        nbytes=D * HID,
    )(place, x_own, panels)[0]


def packed_dx(dpre_ref, owned_ref, out_ref):
    out_t = out_ref.dtype
    first = CHIPS * LANES
    wide = matmul(dpre_ref[...], owned_ref[:first, :], 1, 1)
    narrow = matmul(dpre_ref[...], owned_ref[first:, :], 1, 1)
    left = lax.broadcasted_iota(jnp.int32, (EXPERTS, CAP // 2, LANES), 2) < REST
    for j in range(CHIPS):
        part = wide[:, j * LANES : (j + 1) * LANES].astype(out_t)
        out_ref[:, j, 0:CAP, :] = part.reshape(EXPERTS, CAP, LANES)
    for m in range(CHIPS // 2):
        here = narrow[:, m * LANES : (m + 1) * LANES]
        there = pltpu.roll(here, REST, 1)
        here = here.reshape(EXPERTS, CAP, LANES)
        there = there.reshape(EXPERTS, CAP, LANES)
        lo, hi = slice(0, CAP // 2), slice(CAP // 2, CAP)
        even = jnp.where(left, here[:, lo, :], there[:, hi, :])
        odd = jnp.where(left, there[:, lo, :], here[:, hi, :])
        out_ref[:, 2 * m, CAP:PACK, :] = even.astype(out_t)
        out_ref[:, 2 * m + 1, CAP:PACK, :] = odd.astype(out_t)


def middle(place, part, x_oth, back, panels):
    def body(place_ref, part_ref, oth_ref, back_ref, panel_ref, hid_ref, dpre_ref, dx_ref, *tmp):
        up, owned, up_sems, sems = tmp
        other = 1 - place_ref[0]
        ups = half_rows(panel_ref, other, up, up_sems)
        copies = owned_rows(panel_ref, other, owned, sems)
        for c in ups:
            c.wait()
        pre = part_ref[...] + matmul(oth_ref[...], up[...], 1, 0)
        sig = jax.nn.sigmoid(pre)
        hid_ref[...] = (pre * sig).astype(BF)
        dpre_ref[...] = (back_ref[...] * sig * (1.0 + pre * (1.0 - sig))).astype(BF)
        for c in copies:
            c.wait()
        packed_dx(dpre_ref, owned, dx_ref)

    half = pltpu.VMEM((HALF, HID), BF)
    return call(
        body,
        [SM, VM, VM, VM, HB],
        [((ROWS, HID), BF), ((ROWS, HID), BF), ((EXPERTS, CHIPS, PACK, LANES), BF)],
        [half, half, DMA((PARTS,)), DMA((2 * CHIPS,))],
        limit=TIGHT,
        flops=2 * ROWS * D * HID,
        nbytes=2 * D * HID,
    )(place, part, x_oth, back, panels)


def dx_mine(place, d_pre, panels):
    def body(place_ref, dpre_ref, panel_ref, dx_ref, owned, sems):
        for c in owned_rows(panel_ref, place_ref[0], owned, sems):
            c.wait()
        packed_dx(dpre_ref, owned, dx_ref)

    return call(
        body,
        [SM, VM, HB],
        [((EXPERTS, CHIPS, PACK, LANES), F32)],
        [pltpu.VMEM((HALF, HID), BF), DMA((2 * CHIPS,))],
        limit=TIGHT,
        flops=ROWS * D * HID,
        nbytes=D * HID,
    )(place, d_pre, panels)[0]


def weight_grads(place, own, oth, right, which, step, block, into=None):
    steps = HALF // step

    def body(place_ref, own_ref, oth_ref, right_ref, *rest):
        out_ref = rest[-1]
        k = pl.program_id(0)

        @pl.when(k < steps)
        def _():
            out_ref[0, 0] = matmul(own_ref[...], right_ref[...], 0, 0) * (1.0 / EXPERTS)

        @pl.when(k >= steps)
        def _():
            out_ref[0, 0] = matmul(oth_ref[...], right_ref[...], 0, 0) * (1.0 / EXPERTS)

    def target(k, p):
        side, k = k // steps, k % steps
        return (0, which, ((p[0] + side) % 2) * steps + block(k, p), 0)

    extra = [] if into is None else [into]
    return pl.pallas_call(
        body,
        grid_spec=pltpu.PrefetchScalarGridSpec(
            num_scalar_prefetch=1,
            grid=(2 * steps,),
            in_specs=[
                pl.BlockSpec((ROWS, step), lambda k, p: (0, jnp.minimum(k, steps - 1))),
                pl.BlockSpec((ROWS, step), lambda k, p: (0, jnp.clip(k - steps, 0, steps - 1))),
                pl.BlockSpec((ROWS, HID), lambda k, p: (0, 0)),
            ]
            + [ANY] * len(extra),
            out_specs=pl.BlockSpec((1, 1, step, HID), target),
        ),
        out_shape=jax.ShapeDtypeStruct((1, 2, D, HID), F32),
        input_output_aliases={4: 0} if extra else {},
        compiler_params=pltpu.CompilerParams(vmem_limit_bytes=20 * MIB),
        cost_estimate=pl.CostEstimate(
            flops=2 * ROWS * D * HID, transcendentals=0, bytes_accessed=4 * D * HID
        ),
    )(place, own, oth, right, *extra)


def combine(parts, hot):
    def body(parts_ref, hot_ref, out_ref):
        half = CAP // 2

        def summed(hots, rows):
            return matmul(rows.reshape(-1, LANES), hots.reshape(-1, TOK), 0, 0)

        hot = hot_ref[...].reshape(EXPERTS, 1, CAP, TOK)
        hot = jnp.broadcast_to(hot, (EXPERTS, CHIPS, CAP, TOK))
        parts = parts_ref[...].reshape(EXPERTS, CHIPS, PACK, LANES)
        packed = parts[:, :, CAP:, :]
        out_ref[:LANES, :] = summed(hot, parts[:, :, :CAP, :]).astype(BF)
        low = summed(hot[:, :, :half, :], packed)
        high = summed(hot[:, :, half:, :], packed)
        out_ref[LANES:, :] = (low[:REST, :] + high[REST:, :]).astype(BF)

    return call(body, [VM, VM], [((SLICE, TOK), BF)], [])(parts, hot)[0].T


def shards(tokens, expert_ids, gate_levels, out_grad, panels):
    core, x = lax.axis_index("core"), lax.axis_index("x")
    place = jnp.stack([core, x]).astype(jnp.int32)
    table = jnp.concatenate([expert_ids.T, gate_levels.T], axis=0)
    swap = [(0, 1), (1, 0)]

    def after(value, *deps):
        return lax.optimization_barrier((value,) + deps)[0]

    def exchange(rows, axes):
        return lax.all_to_all(rows, axes, split_axis=0, concat_axis=0, tiled=True)

    grad = lax.dynamic_slice(out_grad, (0, core * HALF + x * QUART), (TOK, QUART))
    d_small = dispatch_d(table, grad).reshape(EXPERTS, CAP, QUART)
    d_first = exchange(d_small, BLK).reshape(ROWS, QUART)
    tok = lax.dynamic_slice(after(tokens, d_small), (0, core * HALF), (TOK, HALF))
    x_rows, hot = dispatch_x(table, tok)
    x_sent = after(x_rows, d_first).reshape(EXPERTS, CAP, HALF)
    x_own = exchange(x_sent, BLK).reshape(ROWS, HALF)
    d_first = after(d_first, x_rows)
    d_own = assemble(
        [d_first]
        + [
            lax.ppermute(d_first, "x", [(i, (i + r) % XS) for i in range(XS)])
            for r in range(1, XS)
        ]
    )
    d_oth = lax.ppermute(d_own, "core", swap)
    back = back_full(place, d_own, d_oth, panels)
    x_oth = lax.ppermute(x_own, "core", swap)
    part = up_own(place, x_own, panels)
    hidden, d_pre, dx_send = middle(place, part, x_oth, back, panels)
    dx_recv = lax.ppermute(dx_send, "core", swap)
    chip_dx = (dx_mine(place, d_pre, panels) + dx_recv.astype(F32)).astype(BF)
    parts = exchange(chip_dx.reshape(DESTS, PACK, LANES), ("yhi", "z", "ylo", "x"))
    step = 512
    panel_grads = weight_grads(
        place, x_own, x_oth, after(d_pre, chip_dx), 0, step, lambda k, p: k
    )
    panel_grads = weight_grads(
        place, d_own, d_oth, hidden, 1, QUART, lambda k, p: (p[1] + XS - k) % XS, panel_grads
    )
    token_grad = combine(after(parts, panel_grads), hot)
    return token_grad, panel_grads


def solution(mesh):
    fine = Mesh(mesh.devices.reshape(SIZES), AXES)
    dp = AXES[:3]
    rows = P(BLK, None)
    return jax.shard_map(
        shards,
        mesh=fine,
        in_specs=(rows, rows, rows, rows, P(BLK, None, None, dp)),
        out_specs=(P(BLK, dp), P(BLK, None, None, dp)),
        check_vma=False,
    )
```

```python
import jax
import jax.numpy as jnp
from jax import lax
from jax.experimental import pallas as pl
from jax.experimental.pallas import tpu as pltpu
from jax.sharding import Mesh, PartitionSpec as P

EXPERTS, CAP, TOK, D, HID = 8, 64, 128, 3072, 512
ROWS = EXPERTS * CAP
HALF = D // 2
XS = 4
QUART = HALF // XS
CHIPS = 8
SLICE = D // (2 * CHIPS)
LANES = 128
REST = SLICE - LANES
PACK = CAP * SLICE // LANES
DESTS = EXPERTS * CHIPS
BF, F32 = jnp.bfloat16, jnp.float32
BLK = ("yhi", "z")
AXES = ("ylo", "x", "core", "yhi", "z")
SIZES = (2, 4, 2, 2, 4)
MIB = 1024 * 1024


def matmul(a, b, ca, cb):
    return lax.dot_general(a, b, (((ca,), (cb,)), ((), ())), preferred_element_type=F32)


VM = pl.BlockSpec(memory_space=pltpu.VMEM)
SM = pl.BlockSpec(memory_space=pltpu.SMEM)
HB = pl.BlockSpec(memory_space=pltpu.HBM)
ANY = pl.BlockSpec(memory_space=pl.ANY)
DMA = pltpu.SemaphoreType.DMA


def call(body, ins, outs, scratch, limit=20, flops=0, nbytes=0, **kw):
    return pl.pallas_call(
        body,
        in_specs=ins,
        out_specs=[VM] * len(outs),
        out_shape=[jax.ShapeDtypeStruct(s, t) for s, t in outs],
        scratch_shapes=scratch,
        compiler_params=pltpu.CompilerParams(vmem_limit_bytes=limit * MIB),
        cost_estimate=pl.CostEstimate(flops=flops, transcendentals=0, bytes_accessed=nbytes),
        **kw,
    )


def slot_rows(table):
    expert = lax.broadcasted_iota(jnp.int32, (EXPERTS, TOK), 0)
    chosen = (expert == table[0:1, :]) | (expert == table[1:2, :])
    before = lax.broadcasted_iota(jnp.int32, (TOK, TOK), 0) < lax.broadcasted_iota(
        jnp.int32, (TOK, TOK), 1
    )
    earlier = matmul(
        jnp.where(chosen, 1.0, 0.0).astype(BF), jnp.where(before, 1.0, 0.0).astype(BF), 1, 0
    )
    return expert, jnp.where(chosen, earlier, -1.0)


def hot_chunk(slot, e):
    place = lax.broadcasted_iota(jnp.int32, (CAP, TOK), 0).astype(F32)
    return jnp.where(place == slot[e : e + 1, :], 1.0, 0.0).astype(F32)


def dispatch_x(table, tokens):
    def body(table_ref, tok_ref, out_ref, hot_ref):
        _, slot = slot_rows(table_ref[...])
        for e in range(EXPERTS):
            hot_ref[e * CAP : (e + 1) * CAP, :] = hot_chunk(slot, e).astype(BF)
        out_ref[...] = matmul(hot_ref[...], tok_ref[...], 1, 0).astype(BF)

    return call(body, [VM, VM], [((ROWS, HALF), BF), ((ROWS, TOK), BF)], [])(table, tokens)


def dispatch_d(table, out_grad):
    def body(table_ref, grad_ref, out_ref, hot_ref, gate_ref):
        table = table_ref[...]
        expert, slot = slot_rows(table)
        lev = table[2:4, :].astype(F32)
        frac = lev / (lev[0:1, :] + lev[1:2, :])
        frac = jnp.where(
            expert == table[0:1, :],
            frac[0:1, :],
            jnp.where(expert == table[1:2, :], frac[1:2, :], 0.0),
        )
        for e in range(EXPERTS):
            rows = slice(e * CAP, (e + 1) * CAP)
            hot = hot_chunk(slot, e)
            hot_ref[rows, :] = hot.astype(BF)
            gate = jnp.sum(hot * frac[e : e + 1, :], axis=1, keepdims=True)
            gate_ref[rows, :] = jnp.broadcast_to(gate, (CAP, LANES))
        rows = matmul(hot_ref[...], grad_ref[...], 1, 0)
        out_ref[...] = (rows * gate_ref[:, 0:1]).astype(BF)

    return call(
        body,
        [VM, VM],
        [((ROWS, QUART), BF)],
        [pltpu.VMEM((ROWS, TOK), BF), pltpu.VMEM((ROWS, LANES), F32)],
    )(table, out_grad)[0]


def assemble(place, pieces):
    def body(place_ref, *refs):
        for r in range(XS):
            start = ((place_ref[1] + XS - r) % XS) * QUART
            refs[XS][:, pl.ds(pl.multiple_of(start, LANES), QUART)] = refs[r][...]

    return call(body, [SM] + [VM] * XS, [((ROWS, HALF), BF)], [])(place, *pieces)[0]


def half_of(panel_ref, which, half):
    return panel_ref[0, which, pl.ds(pl.multiple_of(half * HALF, HALF), HALF), :]


def owned_rows(panel_ref, o, buf):
    for j in range(CHIPS):
        first = pl.multiple_of((2 * j + o) * SLICE, SLICE)
        into = CHIPS * LANES + j * REST
        buf[j * LANES : (j + 1) * LANES, :] = panel_ref[0, 0, pl.ds(first, LANES), :]
        rest = pl.multiple_of(first + LANES, REST)
        buf[into : into + REST, :] = panel_ref[0, 0, pl.ds(rest, REST), :]


def back_full(place, d_own, d_oth, panels):
    def body(place_ref, own_ref, oth_ref, panel_ref, out_ref):
        core = place_ref[0]
        own = matmul(own_ref[...], half_of(panel_ref, 1, core), 1, 0)
        out_ref[...] = own + matmul(oth_ref[...], half_of(panel_ref, 1, 1 - core), 1, 0)

    return call(
        body,
        [SM, VM, VM, VM],
        [((ROWS, HID), F32)],
        [],
        flops=2 * ROWS * D * HID,
        nbytes=2 * D * HID,
    )(place, d_own, d_oth, panels)[0]


def up_own(place, x_own, panels):
    def body(place_ref, own_ref, panel_ref, out_ref):
        out_ref[...] = matmul(own_ref[...], half_of(panel_ref, 0, place_ref[0]), 1, 0)

    return call(
        body, [SM, VM, VM], [((ROWS, HID), F32)], [], flops=ROWS * D * HID, nbytes=D * HID
    )(place, x_own, panels)[0]


def packed_dx(dpre_ref, owned_ref, out_ref):
    out_t = out_ref.dtype
    first = CHIPS * LANES
    wide = matmul(dpre_ref[...], owned_ref[:first, :], 1, 1)
    narrow = matmul(dpre_ref[...], owned_ref[first:, :], 1, 1)
    left = lax.broadcasted_iota(jnp.int32, (EXPERTS, CAP // 2, LANES), 2) < REST
    for j in range(CHIPS):
        part = wide[:, j * LANES : (j + 1) * LANES].astype(out_t)
        out_ref[:, j, 0:CAP, :] = part.reshape(EXPERTS, CAP, LANES)
    for m in range(CHIPS // 2):
        here = narrow[:, m * LANES : (m + 1) * LANES]
        there = pltpu.roll(here, REST, 1)
        here = here.reshape(EXPERTS, CAP, LANES)
        there = there.reshape(EXPERTS, CAP, LANES)
        lo, hi = slice(0, CAP // 2), slice(CAP // 2, CAP)
        even = jnp.where(left, here[:, lo, :], there[:, hi, :])
        odd = jnp.where(left, there[:, lo, :], here[:, hi, :])
        out_ref[:, 2 * m, CAP:PACK, :] = even.astype(out_t)
        out_ref[:, 2 * m + 1, CAP:PACK, :] = odd.astype(out_t)


def middle(place, part, x_oth, back, panels):
    def body(place_ref, part_ref, oth_ref, back_ref, panel_ref, hid_ref, dpre_ref, dx_ref, owned):
        other = 1 - place_ref[0]
        pre = part_ref[...] + matmul(oth_ref[...], half_of(panel_ref, 0, other), 1, 0)
        owned_rows(panel_ref, other, owned)
        sig = jax.nn.sigmoid(pre)
        hid_ref[...] = (pre * sig).astype(BF)
        dpre_ref[...] = (back_ref[...] * sig * (1.0 + pre * (1.0 - sig))).astype(BF)
        packed_dx(dpre_ref, owned, dx_ref)

    return call(
        body,
        [SM, VM, VM, VM, VM],
        [((ROWS, HID), BF), ((ROWS, HID), BF), ((EXPERTS, CHIPS, PACK, LANES), BF)],
        [pltpu.VMEM((HALF, HID), BF)],
        flops=2 * ROWS * D * HID,
        nbytes=2 * D * HID,
    )(place, part, x_oth, back, panels)


def dx_mine(place, d_pre, panels):
    def body(place_ref, dpre_ref, panel_ref, dx_ref, owned):
        owned_rows(panel_ref, place_ref[0], owned)
        packed_dx(dpre_ref, owned, dx_ref)

    return call(
        body,
        [SM, VM, VM],
        [((EXPERTS, CHIPS, PACK, LANES), F32)],
        [pltpu.VMEM((HALF, HID), BF)],
        flops=ROWS * D * HID,
        nbytes=D * HID,
    )(place, d_pre, panels)[0]


def weight_grads(place, own, oth, right, which, into=None):
    step = 512
    steps = HALF // step

    def body(place_ref, own_ref, oth_ref, right_ref, *rest):
        out_ref = rest[-1]
        k = pl.program_id(0)

        @pl.when(k < steps)
        def _():
            out_ref[0, 0] = matmul(own_ref[...], right_ref[...], 0, 0) * (1.0 / EXPERTS)

        @pl.when(k >= steps)
        def _():
            out_ref[0, 0] = matmul(oth_ref[...], right_ref[...], 0, 0) * (1.0 / EXPERTS)

    def target(k, p):
        side, k = k // steps, k % steps
        return (0, which, ((p[0] + side) % 2) * steps + k, 0)

    extra = [] if into is None else [into]
    return pl.pallas_call(
        body,
        grid_spec=pltpu.PrefetchScalarGridSpec(
            num_scalar_prefetch=1,
            grid=(2 * steps,),
            in_specs=[
                pl.BlockSpec((ROWS, step), lambda k, p: (0, jnp.minimum(k, steps - 1))),
                pl.BlockSpec((ROWS, step), lambda k, p: (0, jnp.clip(k - steps, 0, steps - 1))),
                pl.BlockSpec((ROWS, HID), lambda k, p: (0, 0)),
            ]
            + [ANY] * len(extra),
            out_specs=pl.BlockSpec((1, 1, step, HID), target),
        ),
        out_shape=jax.ShapeDtypeStruct((1, 2, D, HID), F32),
        input_output_aliases={4: 0} if extra else {},
        compiler_params=pltpu.CompilerParams(vmem_limit_bytes=20 * MIB),
        cost_estimate=pl.CostEstimate(
            flops=2 * ROWS * D * HID, transcendentals=0, bytes_accessed=4 * D * HID
        ),
    )(place, own, oth, right, *extra)


def combine(parts, hot):
    def body(parts_ref, hot_ref, out_ref):
        half = CAP // 2

        def summed(hots, rows):
            return matmul(rows.reshape(-1, LANES), hots.reshape(-1, TOK), 0, 0)

        hot = hot_ref[...].reshape(EXPERTS, 1, CAP, TOK)
        hot = jnp.broadcast_to(hot, (EXPERTS, CHIPS, CAP, TOK))
        parts = parts_ref[...].reshape(EXPERTS, CHIPS, PACK, LANES)
        packed = parts[:, :, CAP:, :]
        out_ref[:LANES, :] = summed(hot, parts[:, :, :CAP, :]).astype(BF)
        low = summed(hot[:, :, :half, :], packed)
        high = summed(hot[:, :, half:, :], packed)
        out_ref[LANES:, :] = (low[:REST, :] + high[REST:, :]).astype(BF)

    return call(body, [VM, VM], [((SLICE, TOK), BF)], [])(parts, hot)[0].T


def shards(tokens, expert_ids, gate_levels, out_grad, panels):
    core, x = lax.axis_index("core"), lax.axis_index("x")
    place = jnp.stack([core, x]).astype(jnp.int32)
    table = jnp.concatenate([expert_ids.T, gate_levels.T], axis=0)
    swap = [(0, 1), (1, 0)]

    def after(value, *deps):
        return lax.optimization_barrier((value,) + deps)[0]

    def exchange(rows, axes):
        return lax.all_to_all(rows, axes, split_axis=0, concat_axis=0, tiled=True)

    grad = lax.dynamic_slice(out_grad, (0, core * HALF + x * QUART), (TOK, QUART))
    d_small = dispatch_d(table, grad).reshape(EXPERTS, CAP, QUART)
    d_first = exchange(d_small, BLK).reshape(ROWS, QUART)
    tok = lax.dynamic_slice(after(tokens, d_small), (0, core * HALF), (TOK, HALF))
    x_rows, hot = dispatch_x(table, tok)
    x_sent = after(x_rows, d_first).reshape(EXPERTS, CAP, HALF)
    x_own = exchange(x_sent, BLK).reshape(ROWS, HALF)
    d_first = after(d_first, x_rows)
    d_own = assemble(
        place,
        [d_first]
        + [
            lax.ppermute(d_first, "x", [(i, (i + r) % XS) for i in range(XS)])
            for r in range(1, XS)
        ],
    )
    d_oth = lax.ppermute(d_own, "core", swap)
    back = back_full(place, d_own, d_oth, panels)
    x_oth = lax.ppermute(x_own, "core", swap)
    part = up_own(place, x_own, panels)
    hidden, d_pre, dx_send = middle(place, part, x_oth, back, panels)
    dx_recv = lax.ppermute(dx_send, "core", swap)
    chip_dx = (dx_mine(place, d_pre, panels) + dx_recv.astype(F32)).astype(BF)
    parts = exchange(chip_dx.reshape(DESTS, PACK, LANES), ("yhi", "z", "ylo", "x"))
    panel_grads = weight_grads(place, x_own, x_oth, after(d_pre, chip_dx), 0)
    panel_grads = weight_grads(place, d_own, d_oth, hidden, 1, panel_grads)
    token_grad = combine(after(parts, panel_grads), hot)
    return token_grad, panel_grads


def solution(mesh):
    fine = Mesh(mesh.devices.reshape(SIZES), AXES)
    dp = AXES[:3]
    rows = P(BLK, None)
    return jax.shard_map(
        shards,
        mesh=fine,
        in_specs=(rows, rows, rows, rows, P(BLK, None, None, dp)),
        out_specs=(P(BLK, dp), P(BLK, None, None, dp)),
        check_vma=False,
    )
```

```python
import itertools

import jax
import jax.numpy as jnp
from jax import lax
from jax.experimental import pallas as pl
from jax.experimental.pallas import tpu as pltpu
from jax.sharding import Mesh, PartitionSpec as P

EXPERTS, CAP, TOK, D, HID = 8, 64, 128, 3072, 512
ROWS = EXPERTS * CAP
HALF = D // 2
XS = 4
QUART = HALF // XS
CHIPS = 8
SLICE = D // (2 * CHIPS)
LANES = 128
REST = SLICE - LANES
PACK = CAP * SLICE // LANES
DESTS = EXPERTS * CHIPS
BF, F32 = jnp.bfloat16, jnp.float32
BLK = ("yhi", "z")
AXES = ("ylo", "x", "core", "yhi", "z")
SIZES = (2, 4, 2, 2, 4)

SHIFTS = ((0, 0), (0, 1), (0, 3), (1, 2), (1, 1), (1, 3), (0, 2), (1, 0))
MIB = 1024 * 1024


def moves(flip, dz):
    def flat(place):
        number = 0
        for part, size in zip(place, SIZES):
            number = number * size + part
        return number

    return [
        (flat((yl, x, c, yh, z)), flat((yl ^ flip, x, c, yh ^ flip, (z + dz) % 4)))
        for yl, x, c, yh, z in itertools.product(*map(range, SIZES))
    ]


def block_rows(place_ref, flip, dz):
    block = ((place_ref[2] + flip) % 2) * 4 + (place_ref[3] + dz) % 4
    return pl.ds(pl.multiple_of(block * CAP, CAP), CAP)


def matmul(a, b, ca, cb):
    return lax.dot_general(a, b, (((ca,), (cb,)), ((), ())), preferred_element_type=F32)


VM = pl.BlockSpec(memory_space=pltpu.VMEM)
SM = pl.BlockSpec(memory_space=pltpu.SMEM)
HB = pl.BlockSpec(memory_space=pltpu.HBM)
ANY = pl.BlockSpec(memory_space=pl.ANY)
DMA = pltpu.SemaphoreType.DMA


def call(body, ins, outs, scratch, limit=20, flops=0, nbytes=0, **kw):
    return pl.pallas_call(
        body,
        in_specs=ins,
        out_specs=[VM] * len(outs),
        out_shape=[jax.ShapeDtypeStruct(s, t) for s, t in outs],
        scratch_shapes=scratch,
        compiler_params=pltpu.CompilerParams(vmem_limit_bytes=limit * MIB),
        cost_estimate=pl.CostEstimate(flops=flops, transcendentals=0, bytes_accessed=nbytes),
        **kw,
    )


def slot_rows(table):
    expert = lax.broadcasted_iota(jnp.int32, (EXPERTS, TOK), 0)
    chosen = (expert == table[0:1, :]) | (expert == table[1:2, :])
    before = lax.broadcasted_iota(jnp.int32, (TOK, TOK), 0) < lax.broadcasted_iota(
        jnp.int32, (TOK, TOK), 1
    )
    earlier = matmul(
        jnp.where(chosen, 1.0, 0.0).astype(BF), jnp.where(before, 1.0, 0.0).astype(BF), 1, 0
    )
    return expert, jnp.where(chosen, earlier, -1.0)


def hot_chunk(slot, e):
    place = lax.broadcasted_iota(jnp.int32, (CAP, TOK), 0).astype(F32)
    return jnp.where(place == slot[e : e + 1, :], 1.0, 0.0).astype(F32)


def dispatch_x(place, table, tokens):
    def body(place_ref, table_ref, tok_ref, *rest):
        outs, hot_ref = rest[:EXPERTS], rest[EXPERTS]
        _, slot = slot_rows(table_ref[...])
        for e in range(EXPERTS):
            hot_ref[e * CAP : (e + 1) * CAP, :] = hot_chunk(slot, e).astype(BF)
        for out_ref, (flip, dz) in zip(outs, SHIFTS):
            hot = hot_ref[block_rows(place_ref, flip, dz), :]
            out_ref[...] = matmul(hot, tok_ref[...], 1, 0).astype(BF)

    outs = [((CAP, HALF), BF)] * EXPERTS + [((ROWS, TOK), BF)]
    return call(body, [SM, VM, VM], outs, [])(place, table, tokens)


def gather_blocks(place, pieces):
    def body(place_ref, *refs):
        for ref, (flip, dz) in zip(refs, SHIFTS):
            refs[EXPERTS][block_rows(place_ref, flip, -dz % 4), :] = ref[...]

    return call(body, [SM] + [VM] * EXPERTS, [((ROWS, HALF), BF)], [])(place, *pieces)[0]


def dispatch_d(table, out_grad):
    def body(table_ref, grad_ref, out_ref, hot_ref, gate_ref):
        table = table_ref[...]
        expert, slot = slot_rows(table)
        lev = table[2:4, :].astype(F32)
        frac = lev / (lev[0:1, :] + lev[1:2, :])
        frac = jnp.where(
            expert == table[0:1, :],
            frac[0:1, :],
            jnp.where(expert == table[1:2, :], frac[1:2, :], 0.0),
        )
        for e in range(EXPERTS):
            rows = slice(e * CAP, (e + 1) * CAP)
            hot = hot_chunk(slot, e)
            hot_ref[rows, :] = hot.astype(BF)
            gate = jnp.sum(hot * frac[e : e + 1, :], axis=1, keepdims=True)
            gate_ref[rows, :] = jnp.broadcast_to(gate, (CAP, LANES))
        rows = matmul(hot_ref[...], grad_ref[...], 1, 0)
        out_ref[...] = (rows * gate_ref[:, 0:1]).astype(BF)

    return call(
        body,
        [VM, VM],
        [((ROWS, QUART), BF)],
        [pltpu.VMEM((ROWS, TOK), BF), pltpu.VMEM((ROWS, LANES), F32)],
    )(table, out_grad)[0]


def assemble(place, mine, left, right, far_top, far_low):
    def body(place_ref, mine_ref, left_ref, right_ref, top_ref, low_ref, out_ref):
        def columns(shift):
            start = ((place_ref[1] + shift) % XS) * QUART
            return pl.ds(pl.multiple_of(start, LANES), QUART)

        out_ref[:, columns(0)] = mine_ref[...]
        out_ref[:, columns(3)] = left_ref[...]
        out_ref[:, columns(1)] = right_ref[...]
        out_ref[: ROWS // 2, columns(2)] = top_ref[...]
        out_ref[ROWS // 2 :, columns(2)] = low_ref[...]

    return call(body, [SM] + [VM] * 5, [((ROWS, HALF), BF)], [])(
        place, mine, left, right, far_top, far_low
    )[0]


def half_of(panel_ref, which, half):
    return panel_ref[0, which, pl.ds(pl.multiple_of(half * HALF, HALF), HALF), :]


def owned_rows(panel_ref, o, buf):
    for j in range(CHIPS):
        first = pl.multiple_of((2 * j + o) * SLICE, SLICE)
        into = CHIPS * LANES + j * REST
        buf[j * LANES : (j + 1) * LANES, :] = panel_ref[0, 0, pl.ds(first, LANES), :]
        rest = pl.multiple_of(first + LANES, REST)
        buf[into : into + REST, :] = panel_ref[0, 0, pl.ds(rest, REST), :]


def back_full(place, d_own, d_oth, panels):
    def body(place_ref, own_ref, oth_ref, panel_ref, out_ref):
        core = place_ref[0]
        own = matmul(own_ref[...], half_of(panel_ref, 1, core), 1, 0)
        out_ref[...] = own + matmul(oth_ref[...], half_of(panel_ref, 1, 1 - core), 1, 0)

    return call(
        body,
        [SM, VM, VM, VM],
        [((ROWS, HID), F32)],
        [],
        flops=2 * ROWS * D * HID,
        nbytes=2 * D * HID,
    )(place, d_own, d_oth, panels)[0]


def up_own(place, x_own, panels):
    def body(place_ref, own_ref, panel_ref, out_ref):
        out_ref[...] = matmul(own_ref[...], half_of(panel_ref, 0, place_ref[0]), 1, 0)

    return call(
        body, [SM, VM, VM], [((ROWS, HID), F32)], [], flops=ROWS * D * HID, nbytes=D * HID
    )(place, x_own, panels)[0]


def packed_dx(dpre_ref, owned_ref, out_ref):
    out_t = out_ref.dtype
    first = CHIPS * LANES
    wide = matmul(dpre_ref[...], owned_ref[:first, :], 1, 1)
    narrow = matmul(dpre_ref[...], owned_ref[first:, :], 1, 1)
    left = lax.broadcasted_iota(jnp.int32, (EXPERTS, CAP // 2, LANES), 2) < REST
    for j in range(CHIPS):
        part = wide[:, j * LANES : (j + 1) * LANES].astype(out_t)
        out_ref[:, j, 0:CAP, :] = part.reshape(EXPERTS, CAP, LANES)
    for m in range(CHIPS // 2):
        here = narrow[:, m * LANES : (m + 1) * LANES]
        there = pltpu.roll(here, REST, 1)
        here = here.reshape(EXPERTS, CAP, LANES)
        there = there.reshape(EXPERTS, CAP, LANES)
        lo, hi = slice(0, CAP // 2), slice(CAP // 2, CAP)
        even = jnp.where(left, here[:, lo, :], there[:, hi, :])
        odd = jnp.where(left, there[:, lo, :], here[:, hi, :])
        out_ref[:, 2 * m, CAP:PACK, :] = even.astype(out_t)
        out_ref[:, 2 * m + 1, CAP:PACK, :] = odd.astype(out_t)


def middle(place, part, x_oth, back, panels):
    def body(place_ref, part_ref, oth_ref, back_ref, panel_ref, hid_ref, dpre_ref, dx_ref, owned):
        other = 1 - place_ref[0]
        pre = part_ref[...] + matmul(oth_ref[...], half_of(panel_ref, 0, other), 1, 0)
        owned_rows(panel_ref, other, owned)
        sig = jax.nn.sigmoid(pre)
        hid_ref[...] = (pre * sig).astype(BF)
        dpre_ref[...] = (back_ref[...] * sig * (1.0 + pre * (1.0 - sig))).astype(BF)
        packed_dx(dpre_ref, owned, dx_ref)

    return call(
        body,
        [SM, VM, VM, VM, VM],
        [((ROWS, HID), BF), ((ROWS, HID), BF), ((EXPERTS, CHIPS, PACK, LANES), BF)],
        [pltpu.VMEM((HALF, HID), BF)],
        flops=2 * ROWS * D * HID,
        nbytes=2 * D * HID,
    )(place, part, x_oth, back, panels)


def dx_mine(place, d_pre, panels):
    def body(place_ref, dpre_ref, panel_ref, dx_ref, owned):
        owned_rows(panel_ref, place_ref[0], owned)
        packed_dx(dpre_ref, owned, dx_ref)

    return call(
        body,
        [SM, VM, VM],
        [((EXPERTS, CHIPS, PACK, LANES), F32)],
        [pltpu.VMEM((HALF, HID), BF)],
        flops=ROWS * D * HID,
        nbytes=D * HID,
    )(place, d_pre, panels)[0]


def weight_grads(place, own, oth, right, which, into=None):
    step = 512
    steps = HALF // step

    def body(place_ref, own_ref, oth_ref, right_ref, *rest):
        out_ref = rest[-1]
        k = pl.program_id(0)

        @pl.when(k < steps)
        def _():
            out_ref[0, 0] = matmul(own_ref[...], right_ref[...], 0, 0) * (1.0 / EXPERTS)

        @pl.when(k >= steps)
        def _():
            out_ref[0, 0] = matmul(oth_ref[...], right_ref[...], 0, 0) * (1.0 / EXPERTS)

    def target(k, p):
        side, k = k // steps, k % steps
        return (0, which, ((p[0] + side) % 2) * steps + k, 0)

    extra = [] if into is None else [into]
    return pl.pallas_call(
        body,
        grid_spec=pltpu.PrefetchScalarGridSpec(
            num_scalar_prefetch=1,
            grid=(2 * steps,),
            in_specs=[
                pl.BlockSpec((ROWS, step), lambda k, p: (0, jnp.minimum(k, steps - 1))),
                pl.BlockSpec((ROWS, step), lambda k, p: (0, jnp.clip(k - steps, 0, steps - 1))),
                pl.BlockSpec((ROWS, HID), lambda k, p: (0, 0)),
            ]
            + [ANY] * len(extra),
            out_specs=pl.BlockSpec((1, 1, step, HID), target),
        ),
        out_shape=jax.ShapeDtypeStruct((1, 2, D, HID), F32),
        input_output_aliases={4: 0} if extra else {},
        compiler_params=pltpu.CompilerParams(vmem_limit_bytes=20 * MIB),
        cost_estimate=pl.CostEstimate(
            flops=2 * ROWS * D * HID, transcendentals=0, bytes_accessed=4 * D * HID
        ),
    )(place, own, oth, right, *extra)


def combine(parts, hot):
    def body(parts_ref, hot_ref, out_ref):
        half = CAP // 2

        def summed(hots, rows):
            hots, rows = hots.reshape(-1, TOK), rows.reshape(-1, LANES)
            high = rows.astype(BF)
            low = (rows - high.astype(F32)).astype(BF)
            return matmul(high, hots, 0, 0) + matmul(low, hots, 0, 0)

        parts = parts_ref[...].reshape(EXPERTS, CHIPS, PACK, LANES)
        total = parts[:, 0].astype(F32)
        for j in range(1, CHIPS):
            total += parts[:, j].astype(F32)
        hot = hot_ref[...].reshape(EXPERTS, CAP, TOK)
        out_ref[:LANES, :] = summed(hot, total[:, :CAP, :]).astype(BF)
        low = summed(hot[:, :half, :], total[:, CAP:, :])
        high = summed(hot[:, half:, :], total[:, CAP:, :])
        out_ref[LANES:, :] = (low[:REST, :] + high[REST:, :]).astype(BF)

    return call(body, [VM, VM], [((SLICE, TOK), BF)], [])(parts, hot)[0].T


def shards(tokens, expert_ids, gate_levels, out_grad, panels):
    core, x = lax.axis_index("core"), lax.axis_index("x")
    place = [core, x, lax.axis_index("yhi"), lax.axis_index("z")]
    place = jnp.stack(place).astype(jnp.int32)
    table = jnp.concatenate([expert_ids.T, gate_levels.T], axis=0)
    swap = [(0, 1), (1, 0)]

    def after(value, *deps):
        return lax.optimization_barrier((value,) + deps)[0]

    def exchange(rows, axes):
        return lax.all_to_all(rows, axes, split_axis=0, concat_axis=0, tiled=True)

    grad = lax.dynamic_slice(out_grad, (0, core * HALF + x * QUART), (TOK, QUART))
    d_small = dispatch_d(table, grad).reshape(EXPERTS, CAP, QUART)
    d_first = exchange(d_small, BLK).reshape(ROWS, QUART)
    tok = lax.dynamic_slice(after(tokens, d_small), (0, core * HALF), (TOK, HALF))
    *x_msgs, hot = dispatch_x(place, table, tok)

    def send_x(k, *deps):
        piece = after(x_msgs[k], *deps) if deps else x_msgs[k]
        return lax.ppermute(piece, AXES, moves(*SHIFTS[k]))

    got = [x_msgs[0]] + [send_x(k) for k in (1, 2, 3)]
    up_x = [(i, (i + 1) % XS) for i in range(XS)]
    down_x = [(i, (i - 1) % XS) for i in range(XS)]
    d_first = after(d_first, got[1])
    left, right = lax.ppermute(d_first, "x", up_x), lax.ppermute(d_first, "x", down_x)
    for k in (4, 5, 6, 7):
        got.append(send_x(k, got[k - 3]))
    far_top = lax.ppermute(right[: ROWS // 2], "x", down_x)
    far_low = lax.ppermute(left[ROWS // 2 :], "x", up_x)
    x_own = gather_blocks(place, got)
    d_own = assemble(place, d_first, left, right, far_top, far_low)
    d_oth = lax.ppermute(d_own, "core", swap)
    back = back_full(place, d_own, d_oth, panels)
    x_oth = lax.ppermute(x_own, "core", swap)
    part = up_own(place, x_own, panels)
    hidden, d_pre, dx_send = middle(place, part, x_oth, back, panels)
    dx_recv = lax.ppermute(dx_send, "core", swap)
    chip_dx = (dx_mine(place, d_pre, panels) + dx_recv.astype(F32)).astype(BF)
    parts = exchange(chip_dx.reshape(DESTS, PACK, LANES), ("yhi", "z", "ylo", "x"))
    panel_grads = weight_grads(place, x_own, x_oth, after(d_pre, chip_dx), 0)
    panel_grads = weight_grads(place, d_own, d_oth, hidden, 1, panel_grads)
    token_grad = combine(after(parts, panel_grads), hot)
    return token_grad, panel_grads


def solution(mesh):
    fine = Mesh(mesh.devices.reshape(SIZES), AXES)
    dp = AXES[:3]
    rows = P(BLK, None)
    return jax.shard_map(
        shards,
        mesh=fine,
        in_specs=(rows, rows, rows, rows, P(BLK, None, None, dp)),
        out_specs=(P(BLK, dp), P(BLK, None, None, dp)),
        check_vma=False,
    )
```

```python
import itertools

import jax
import jax.numpy as jnp
from jax import lax
from jax.experimental import pallas as pl
from jax.experimental.pallas import tpu as pltpu
from jax.sharding import Mesh, PartitionSpec as P

EXPERTS, CAP, TOK, D, HID = 8, 64, 128, 3072, 512
ROWS = EXPERTS * CAP
HALF = D // 2
XS = 4
QUART = HALF // XS
CHIPS = 8
SLICE = D // (2 * CHIPS)
LANES = 128
REST = SLICE - LANES
PACK = CAP * SLICE // LANES
DESTS = EXPERTS * CHIPS
BF, F32 = jnp.bfloat16, jnp.float32
BLK = ("yhi", "z")
AXES = ("ylo", "x", "core", "yhi", "z")
SIZES = (2, 4, 2, 2, 4)

SHIFTS = ((0, 0), (0, 1), (0, 3), (1, 2), (1, 1), (1, 3), (0, 2), (1, 0))
MIB = 1024 * 1024


def moves(flip, dz):
    def flat(place):
        number = 0
        for part, size in zip(place, SIZES):
            number = number * size + part
        return number

    return [
        (flat((yl, x, c, yh, z)), flat((yl ^ flip, x, c, yh ^ flip, (z + dz) % 4)))
        for yl, x, c, yh, z in itertools.product(*map(range, SIZES))
    ]


def block_rows(place_ref, flip, dz):
    block = ((place_ref[2] + flip) % 2) * 4 + (place_ref[3] + dz) % 4
    return pl.ds(pl.multiple_of(block * CAP, CAP), CAP)


def matmul(a, b, ca, cb):
    return lax.dot_general(a, b, (((ca,), (cb,)), ((), ())), preferred_element_type=F32)


VM = pl.BlockSpec(memory_space=pltpu.VMEM)
SM = pl.BlockSpec(memory_space=pltpu.SMEM)
HB = pl.BlockSpec(memory_space=pltpu.HBM)
ANY = pl.BlockSpec(memory_space=pl.ANY)
DMA = pltpu.SemaphoreType.DMA


def call(body, ins, outs, scratch, limit=20, flops=0, nbytes=0, **kw):
    return pl.pallas_call(
        body,
        in_specs=ins,
        out_specs=[VM] * len(outs),
        out_shape=[jax.ShapeDtypeStruct(s, t) for s, t in outs],
        scratch_shapes=scratch,
        compiler_params=pltpu.CompilerParams(vmem_limit_bytes=limit * MIB),
        cost_estimate=pl.CostEstimate(flops=flops, transcendentals=0, bytes_accessed=nbytes),
        **kw,
    )


def slot_rows(table):
    expert = lax.broadcasted_iota(jnp.int32, (EXPERTS, TOK), 0)
    chosen = (expert == table[0:1, :]) | (expert == table[1:2, :])
    before = lax.broadcasted_iota(jnp.int32, (TOK, TOK), 0) < lax.broadcasted_iota(
        jnp.int32, (TOK, TOK), 1
    )
    earlier = matmul(
        jnp.where(chosen, 1.0, 0.0).astype(BF), jnp.where(before, 1.0, 0.0).astype(BF), 1, 0
    )
    return expert, jnp.where(chosen, earlier, -1.0)


def hot_chunk(slot, e):
    place = lax.broadcasted_iota(jnp.int32, (CAP, TOK), 0).astype(F32)
    return jnp.where(place == slot[e : e + 1, :], 1.0, 0.0).astype(F32)


def dispatch_x(place, table, tokens):
    def body(place_ref, table_ref, tok_ref, *rest):
        outs, hot_ref = rest[:EXPERTS], rest[EXPERTS]
        _, slot = slot_rows(table_ref[...])
        for e in range(EXPERTS):
            hot_ref[e * CAP : (e + 1) * CAP, :] = hot_chunk(slot, e).astype(BF)
        for out_ref, (flip, dz) in zip(outs, SHIFTS):
            hot = hot_ref[block_rows(place_ref, flip, dz), :]
            out_ref[...] = matmul(hot, tok_ref[...], 1, 0).astype(BF)

    outs = [((CAP, HALF), BF)] * EXPERTS + [((ROWS, TOK), BF)]
    return call(body, [SM, VM, VM], outs, [])(place, table, tokens)


def gather_blocks(place, pieces):
    def body(place_ref, *refs):
        for ref, (flip, dz) in zip(refs, SHIFTS):
            refs[EXPERTS][block_rows(place_ref, flip, -dz % 4), :] = ref[...]

    return call(body, [SM] + [VM] * EXPERTS, [((ROWS, HALF), BF)], [])(place, *pieces)[0]


def dispatch_d(table, out_grad):
    def body(table_ref, grad_ref, out_ref, hot_ref, gate_ref):
        table = table_ref[...]
        expert, slot = slot_rows(table)
        lev = table[2:4, :].astype(F32)
        frac = lev / (lev[0:1, :] + lev[1:2, :])
        frac = jnp.where(
            expert == table[0:1, :],
            frac[0:1, :],
            jnp.where(expert == table[1:2, :], frac[1:2, :], 0.0),
        )
        for e in range(EXPERTS):
            rows = slice(e * CAP, (e + 1) * CAP)
            hot = hot_chunk(slot, e)
            hot_ref[rows, :] = hot.astype(BF)
            gate = jnp.sum(hot * frac[e : e + 1, :], axis=1, keepdims=True)
            gate_ref[rows, :] = jnp.broadcast_to(gate, (CAP, LANES))
        rows = matmul(hot_ref[...], grad_ref[...], 1, 0)
        out_ref[...] = (rows * gate_ref[:, 0:1]).astype(BF)

    return call(
        body,
        [VM, VM],
        [((ROWS, QUART), BF)],
        [pltpu.VMEM((ROWS, TOK), BF), pltpu.VMEM((ROWS, LANES), F32)],
    )(table, out_grad)[0]


def assemble(place, mine, left, right, far_top, far_low):
    def body(place_ref, mine_ref, left_ref, right_ref, top_ref, low_ref, out_ref):
        def columns(shift):
            start = ((place_ref[1] + shift) % XS) * QUART
            return pl.ds(pl.multiple_of(start, LANES), QUART)

        out_ref[:, columns(0)] = mine_ref[...]
        out_ref[:, columns(3)] = left_ref[...]
        out_ref[:, columns(1)] = right_ref[...]
        out_ref[: ROWS // 2, columns(2)] = top_ref[...]
        out_ref[ROWS // 2 :, columns(2)] = low_ref[...]

    return call(body, [SM] + [VM] * 5, [((ROWS, HALF), BF)], [])(
        place, mine, left, right, far_top, far_low
    )[0]


def half_of(panel_ref, which, half):
    return panel_ref[0, which, pl.ds(pl.multiple_of(half * HALF, HALF), HALF), :]


def owned_rows(panel_ref, o, buf):
    for j in range(CHIPS):
        first = pl.multiple_of((2 * j + o) * SLICE, SLICE)
        into = CHIPS * LANES + j * REST
        buf[j * LANES : (j + 1) * LANES, :] = panel_ref[0, 0, pl.ds(first, LANES), :]
        rest = pl.multiple_of(first + LANES, REST)
        buf[into : into + REST, :] = panel_ref[0, 0, pl.ds(rest, REST), :]


def back_full(place, d_own, d_oth, panels):
    def body(place_ref, own_ref, oth_ref, panel_ref, out_ref):
        core = place_ref[0]
        own = matmul(own_ref[...], half_of(panel_ref, 1, core), 1, 0)
        out_ref[...] = own + matmul(oth_ref[...], half_of(panel_ref, 1, 1 - core), 1, 0)

    return call(
        body,
        [SM, VM, VM, VM],
        [((ROWS, HID), F32)],
        [],
        flops=2 * ROWS * D * HID,
        nbytes=2 * D * HID,
    )(place, d_own, d_oth, panels)[0]


def up_own(place, x_own, panels):
    def body(place_ref, own_ref, panel_ref, out_ref):
        out_ref[...] = matmul(own_ref[...], half_of(panel_ref, 0, place_ref[0]), 1, 0)

    return call(
        body, [SM, VM, VM], [((ROWS, HID), F32)], [], flops=ROWS * D * HID, nbytes=D * HID
    )(place, x_own, panels)[0]


def packed_dx(dpre_ref, owned_ref, out_ref):
    out_t = out_ref.dtype
    first = CHIPS * LANES
    wide = matmul(dpre_ref[...], owned_ref[:first, :], 1, 1)
    narrow = matmul(dpre_ref[...], owned_ref[first:, :], 1, 1)
    left = lax.broadcasted_iota(jnp.int32, (EXPERTS, CAP // 2, LANES), 2) < REST
    for j in range(CHIPS):
        part = wide[:, j * LANES : (j + 1) * LANES].astype(out_t)
        out_ref[:, j, 0:CAP, :] = part.reshape(EXPERTS, CAP, LANES)
    for m in range(CHIPS // 2):
        here = narrow[:, m * LANES : (m + 1) * LANES]
        there = pltpu.roll(here, REST, 1)
        here = here.reshape(EXPERTS, CAP, LANES)
        there = there.reshape(EXPERTS, CAP, LANES)
        lo, hi = slice(0, CAP // 2), slice(CAP // 2, CAP)
        even = jnp.where(left, here[:, lo, :], there[:, hi, :])
        odd = jnp.where(left, there[:, lo, :], here[:, hi, :])
        out_ref[:, 2 * m, CAP:PACK, :] = even.astype(out_t)
        out_ref[:, 2 * m + 1, CAP:PACK, :] = odd.astype(out_t)


def middle(place, part, x_oth, back, panels):
    def body(place_ref, part_ref, oth_ref, back_ref, panel_ref, hid_ref, dpre_ref, dx_ref, owned):
        other = 1 - place_ref[0]
        pre = part_ref[...] + matmul(oth_ref[...], half_of(panel_ref, 0, other), 1, 0)
        owned_rows(panel_ref, other, owned)
        sig = jax.nn.sigmoid(pre)
        hid_ref[...] = (pre * sig).astype(BF)
        dpre_ref[...] = (back_ref[...] * sig * (1.0 + pre * (1.0 - sig))).astype(BF)
        packed_dx(dpre_ref, owned, dx_ref)

    return call(
        body,
        [SM, VM, VM, VM, VM],
        [((ROWS, HID), BF), ((ROWS, HID), BF), ((EXPERTS, CHIPS, PACK, LANES), BF)],
        [pltpu.VMEM((HALF, HID), BF)],
        flops=2 * ROWS * D * HID,
        nbytes=2 * D * HID,
    )(place, part, x_oth, back, panels)


def dx_mine(place, d_pre, panels):
    def body(place_ref, dpre_ref, panel_ref, dx_ref, owned):
        owned_rows(panel_ref, place_ref[0], owned)
        packed_dx(dpre_ref, owned, dx_ref)

    return call(
        body,
        [SM, VM, VM],
        [((EXPERTS, CHIPS, PACK, LANES), BF)],
        [pltpu.VMEM((HALF, HID), BF)],
        flops=ROWS * D * HID,
        nbytes=D * HID,
    )(place, d_pre, panels)[0]


def weight_grads(place, own, oth, right, which, into=None):
    step = 512
    steps = HALF // step

    def body(place_ref, own_ref, oth_ref, right_ref, *rest):
        out_ref = rest[-1]
        k = pl.program_id(0)

        @pl.when(k < steps)
        def _():
            out_ref[0, 0] = matmul(own_ref[...], right_ref[...], 0, 0) * (1.0 / EXPERTS)

        @pl.when(k >= steps)
        def _():
            out_ref[0, 0] = matmul(oth_ref[...], right_ref[...], 0, 0) * (1.0 / EXPERTS)

    def target(k, p):
        side, k = k // steps, k % steps
        return (0, which, ((p[0] + side) % 2) * steps + k, 0)

    extra = [] if into is None else [into]
    return pl.pallas_call(
        body,
        grid_spec=pltpu.PrefetchScalarGridSpec(
            num_scalar_prefetch=1,
            grid=(2 * steps,),
            in_specs=[
                pl.BlockSpec((ROWS, step), lambda k, p: (0, jnp.minimum(k, steps - 1))),
                pl.BlockSpec((ROWS, step), lambda k, p: (0, jnp.clip(k - steps, 0, steps - 1))),
                pl.BlockSpec((ROWS, HID), lambda k, p: (0, 0)),
            ]
            + [ANY] * len(extra),
            out_specs=pl.BlockSpec((1, 1, step, HID), target),
        ),
        out_shape=jax.ShapeDtypeStruct((1, 2, D, HID), F32),
        input_output_aliases={4: 0} if extra else {},
        compiler_params=pltpu.CompilerParams(vmem_limit_bytes=20 * MIB),
        cost_estimate=pl.CostEstimate(
            flops=2 * ROWS * D * HID, transcendentals=0, bytes_accessed=4 * D * HID
        ),
    )(place, own, oth, right, *extra)


def combine(parts, hot):
    def body(parts_ref, hot_ref, out_ref):
        half = CAP // 2

        def summed(hots, rows):
            hots, rows = hots.reshape(-1, TOK), rows.reshape(-1, LANES)
            high = rows.astype(BF)
            low = (rows - high.astype(F32)).astype(BF)
            return matmul(high, hots, 0, 0) + matmul(low, hots, 0, 0)

        parts = parts_ref[...].reshape(EXPERTS, CHIPS, PACK, LANES)
        total = parts[:, 0].astype(F32)
        for j in range(1, CHIPS):
            total += parts[:, j].astype(F32)
        hot = hot_ref[...].reshape(EXPERTS, CAP, TOK)
        out_ref[:LANES, :] = summed(hot, total[:, :CAP, :]).astype(BF)
        low = summed(hot[:, :half, :], total[:, CAP:, :])
        high = summed(hot[:, half:, :], total[:, CAP:, :])
        out_ref[LANES:, :] = (low[:REST, :] + high[REST:, :]).astype(BF)

    return call(body, [VM, VM], [((SLICE, TOK), BF)], [])(parts, hot)[0].T


def shards(tokens, expert_ids, gate_levels, out_grad, panels):
    core, x = lax.axis_index("core"), lax.axis_index("x")
    place = [core, x, lax.axis_index("yhi"), lax.axis_index("z")]
    place = jnp.stack(place).astype(jnp.int32)
    table = jnp.concatenate([expert_ids.T, gate_levels.T], axis=0)
    swap = [(0, 1), (1, 0)]

    def after(value, *deps):
        return lax.optimization_barrier((value,) + deps)[0]

    def exchange(rows, axes):
        return lax.all_to_all(rows, axes, split_axis=0, concat_axis=0, tiled=True)

    grad = lax.dynamic_slice(out_grad, (0, core * HALF + x * QUART), (TOK, QUART))
    d_small = dispatch_d(table, grad).reshape(EXPERTS, CAP, QUART)
    d_first = exchange(d_small, BLK).reshape(ROWS, QUART)
    tok = lax.dynamic_slice(after(tokens, d_small), (0, core * HALF), (TOK, HALF))
    *x_msgs, hot = dispatch_x(place, table, tok)

    def send_x(k, *deps):
        piece = after(x_msgs[k], *deps) if deps else x_msgs[k]
        return lax.ppermute(piece, AXES, moves(*SHIFTS[k]))

    got = [x_msgs[0]] + [send_x(k) for k in (1, 2, 3)]
    up_x = [(i, (i + 1) % XS) for i in range(XS)]
    down_x = [(i, (i - 1) % XS) for i in range(XS)]
    d_first = after(d_first, got[1])
    left, right = lax.ppermute(d_first, "x", up_x), lax.ppermute(d_first, "x", down_x)
    for k in (4, 5, 6, 7):
        got.append(send_x(k, got[k - 3]))
    far_top = lax.ppermute(right[: ROWS // 2], "x", down_x)
    far_low = lax.ppermute(left[ROWS // 2 :], "x", up_x)
    x_own = gather_blocks(place, got)
    d_own = assemble(place, d_first, left, right, far_top, far_low)
    d_oth = lax.ppermute(d_own, "core", swap)
    back = back_full(place, d_own, d_oth, panels)
    x_oth = lax.ppermute(x_own, "core", swap)
    part = up_own(place, x_own, panels)
    hidden, d_pre, dx_send = middle(place, part, x_oth, back, panels)
    dx_recv = lax.ppermute(dx_send, "core", swap)
    chip_dx = (dx_mine(place, d_pre, panels).astype(F32) + dx_recv.astype(F32)).astype(BF)
    parts = exchange(chip_dx.reshape(DESTS, PACK, LANES), ("yhi", "z", "ylo", "x"))
    panel_grads = weight_grads(place, x_own, x_oth, after(d_pre, chip_dx), 0)
    panel_grads = weight_grads(place, d_own, d_oth, hidden, 1, panel_grads)
    token_grad = combine(after(parts, panel_grads), hot)
    return token_grad, panel_grads


def solution(mesh):
    fine = Mesh(mesh.devices.reshape(SIZES), AXES)
    dp = AXES[:3]
    rows = P(BLK, None)
    return jax.shard_map(
        shards,
        mesh=fine,
        in_specs=(rows, rows, rows, rows, P(BLK, None, None, dp)),
        out_specs=(P(BLK, dp), P(BLK, None, None, dp)),
        check_vma=False,
    )
```
